32 devices in a mesh: dp: 8 (over z, x), tensor: 4 (over y, core).
Axes of the slice: x: 2, y: 2, z: 4, core: 2. Of those that a mesh axis runs over, the one named last changes fastest.
Arguments:
- doc_hidden: bfloat16 [4096, 1024], P(('dp', 'tensor')), may hold values from -6 to 6
- query_hidden: bfloat16 [1024, 1024], P(('dp', 'tensor')), may hold values from -6 to 6
- seg_lengths: int32 [8, 4], P('dp'), may hold values from 16 to 128, as said below
- labels: int32 [32], P(('dp', 'tensor')), may hold values from 0 to 31
- w_qkv: bfloat16 [2, 1024, 3, 1024], P(None, None, None, 'tensor'), may hold values from -0.1875 to 0.1875
- b_qkv: float32 [2, 3, 1024], P(None, None, 'tensor'), may hold values from -1.8 to 1.8
- w_attn_out: bfloat16 [2, 1024, 1024], P(None, 'tensor'), may hold values from -1.5 to 1.5
- w_ff_in: bfloat16 [2, 1024, 4096], P(None, None, 'tensor'), may hold values from -0.1875 to 0.1875
- b_ff_in: float32 [2, 4096], P(None, 'tensor'), may hold values from -1.8 to 1.8
- w_ff_out: bfloat16 [2, 4096, 1024], P(None, 'tensor'), may hold values from -0.1875 to 0.1875
- out_bias: float32 [2, 2, 1024], replicated, may hold values from -1.8 to 1.8
- norm_gain: float32 [2, 2, 1024], replicated, may hold values from 0.5 to 1.5
- norm_bias: float32 [2, 2, 1024], replicated, may hold values from -1.2 to 1.2
- w_proj: bfloat16 [1024, 128], replicated, may hold values from -0.1875 to 0.1875
Outputs:
- query_losses: float32 [32], P(('dp', 'tensor'))
- g_doc_hidden: float32 [4096, 1024], P(('dp', 'tensor'))
- g_query_hidden: float32 [1024, 1024], P(('dp', 'tensor'))
- g_w_qkv: float32 [2, 1024, 3, 1024], P(None, 'dp', None, 'tensor')
- g_b_qkv: float32 [2, 3, 1024], P(None, None, ('tensor', 'dp'))
- g_w_attn_out: float32 [2, 1024, 1024], P(None, 'tensor', 'dp')
- g_w_ff_in: float32 [2, 1024, 4096], P(None, 'dp', 'tensor')
- g_b_ff_in: float32 [2, 4096], P(None, ('tensor', 'dp'))
- g_w_ff_out: float32 [2, 4096, 1024], P(None, 'tensor', 'dp')
- g_out_bias: float32 [2, 2, 1024], P(None, None, ('dp', 'tensor'))
- g_norm_gain: float32 [2, 2, 1024], P(None, None, ('dp', 'tensor'))
- g_norm_bias: float32 [2, 2, 1024], P(None, None, ('dp', 'tensor'))
- g_w_proj: float32 [1024, 128], P(('dp', 'tensor'))
The draws below stay inside these ranges and needn't reach their ends.
Inputs may be any that keep to these rules, and one draw needn't show every extreme that they name: `seg_lengths`: each entry is the length of one document of a row, between 16 and 128; every row has an entry equal to 128; a row's entries sum to at most 512, and the rest of the row is padding.
All inputs are finite; a program needn't handle non-finite values.
Results may differ from the reference program's by a relative error of at most 0.024.
Values may be sent and summed in bfloat16 or wider, within the bound.
No kernel may reach another device: no remote copies, remote signals or barrier semaphores. Data moves between devices by JAX's collectives and lax.ppermute only.
A program may use at most 192 MiB of HBM per device.

```python
import math
import jax
import jax.numpy as jnp
from jax import lax

D = 1024
HD = 64
FF = 4096
DIM = 128
LAYERS = 2
ROW = 512
DOCS_ROW = 4
QLEN = 32
MOST = 128
TOKENS = 4096
QUERIES = 32
QTOKENS = 1024
NDOCS = 32
N_DP = 8


def draw_seg_lengths(key, part):
    first, second = jax.random.split(jax.random.fold_in(key, 11))
    values = jax.random.randint(first, (N_DP, DOCS_ROW), max(1, MOST // 8), MOST + 1)
    chosen = jax.random.randint(second, (N_DP, 1), 0, DOCS_ROW)
    column = jnp.arange(DOCS_ROW, dtype=jnp.int32)[None, :]
    return jnp.where(column == chosen, MOST, values).astype(jnp.int32)


def with_ends(drawn, rng, smallest, high):
    shape = drawn.shape
    place = [jax.random.randint(jax.random.fold_in(rng, axis), (), 0, shape[axis]) for axis in range(len(shape))]
    drawn = drawn.at[tuple(place)].set(smallest)
    longest = shape.index(max(shape))
    place[longest] = (place[longest] + 1) % shape[longest]
    return drawn.at[tuple(place)].set(high)


def level_of(own_key, extent, shards, low, high):
    loudness = 1.0
    for axis_at, parts in shards:
        steps = jax.random.uniform(jax.random.fold_in(jax.random.fold_in(own_key, 6), axis_at), (parts,), jnp.float32, low / len(shards), high / len(shards))
        loudness = loudness * jnp.repeat(jnp.exp(steps), extent[axis_at] // parts).reshape((-1,) + (1,) * (len(extent) - 1 - axis_at))
    return loudness


def scatter_about(rng, dims, scale, reach, cuts=(), kind=jnp.bfloat16):
    values = scale * jax.random.normal(rng, dims, jnp.float32)
    if cuts:
        values = values * level_of(rng, dims, cuts, -0.22, 0.18)
    return jnp.clip(values, -reach, reach).astype(kind)


def setup_inputs(seed: int = 0) -> dict:
    seeds = jax.random.split(jax.random.key(seed), 15)
    doc_hidden = scatter_about(seeds[0], (TOKENS, D), 1.0, 6.0, ((0, 32),))
    query_hidden = scatter_about(seeds[1], (QTOKENS, D), 1.0, 6.0, ((0, 32),))
    seg_lengths = draw_seg_lengths(jax.random.fold_in(seeds[14], 71), 0)
    labels = with_ends(jax.random.randint(seeds[3], (QUERIES,), 0, NDOCS), jax.random.fold_in(seeds[3], 1), 0, NDOCS - 1).astype(jnp.int32)
    w_qkv = scatter_about(seeds[4], (LAYERS, D, 3, D), D ** -0.5, 0.1875, ((3, 4),))
    b_qkv = scatter_about(seeds[5], (LAYERS, 3, D), 0.3, 1.8, ((2, 4),), jnp.float32)
    w_attn_out = scatter_about(seeds[6], (LAYERS, D, D), (D // 64) ** -0.5, 1.5, ((1, 4),))
    w_ff_in = scatter_about(seeds[7], (LAYERS, D, FF), D ** -0.5, 0.1875, ((2, 4),))
    b_ff_in = scatter_about(seeds[8], (LAYERS, FF), 0.3, 1.8, ((1, 4),), jnp.float32)
    w_ff_out = scatter_about(seeds[9], (LAYERS, FF, D), (FF // 4) ** -0.5, 0.1875, ((1, 4),))
    out_bias = scatter_about(seeds[10], (LAYERS, 2, D), 0.3, 1.8, (), jnp.float32)
    norm_gain = jnp.clip(1.0 + 0.1 * jax.random.normal(seeds[11], (LAYERS, 2, D), jnp.float32), 0.5, 1.5)
    norm_bias = scatter_about(seeds[12], (LAYERS, 2, D), 0.2, 1.2, (), jnp.float32)
    w_proj = scatter_about(seeds[13], (D, DIM), D ** -0.5, 0.1875)
    return dict(doc_hidden=doc_hidden, query_hidden=query_hidden, seg_lengths=seg_lengths, labels=labels, w_qkv=w_qkv, b_qkv=b_qkv, w_attn_out=w_attn_out, w_ff_in=w_ff_in, b_ff_in=b_ff_in, w_ff_out=w_ff_out, out_bias=out_bias, norm_gain=norm_gain, norm_bias=norm_bias, w_proj=w_proj)


@jax.custom_vjp
def low(v):
    return lax.optimization_barrier(v.astype(jnp.bfloat16)).astype(jnp.float32)

@jax.custom_vjp
def low_back(v):
    return v

def low_keep(v):
    return (low(v), None)

def low_pass(kept, grad):
    return (grad,)

def back_keep(v):
    return (v, None)

def back_low(kept, grad):
    return (low(grad),)
low.defvjp(low_keep, low_pass)
low_back.defvjp(back_keep, back_low)
precise = lax.Precision.HIGHEST
eps_norm = 1e-05
eps_unit = 1e-06
tau_token = 0.1
temp_loss = 0.1
masked_score = -1000000000.0

def matmul(left, right):
    return jnp.dot(left, right, precision=precise, preferred_element_type=jnp.float32)

def layer_norm(values, gain_row, bias_row):
    average = lax.optimization_barrier(jnp.mean(values, axis=-1, keepdims=True))
    centred = values - average
    spread = lax.optimization_barrier(jnp.mean(centred * centred, axis=-1, keepdims=True))
    return centred * lax.rsqrt(spread + eps_norm) * gain_row + bias_row

def unit(values):
    return values * lax.rsqrt(lax.optimization_barrier(jnp.sum(values * values, axis=-1, keepdims=True)) + eps_unit)

def row_layout(lengths, row_len):
    doc_ends = jnp.cumsum(lengths).astype(jnp.int32)
    token_idx = jnp.arange(row_len, dtype=jnp.int32)
    passed = (token_idx[:, None] >= doc_ends[None, :]).astype(jnp.int32)
    segment = lax.optimization_barrier(jnp.sum(passed, axis=1)).astype(jnp.int32)
    starts = lax.optimization_barrier(jnp.sum(passed * lengths[None, :], axis=1)).astype(jnp.int32)
    return (segment, token_idx - starts)

def rotary_tables(positions, head_dim):
    half_dim = head_dim // 2
    frequency = jnp.exp(jnp.arange(half_dim, dtype=jnp.float32) * (-math.log(10000.0) / half_dim))
    angles = positions.astype(jnp.float32)[:, None] * frequency[None, :]
    angles = jnp.concatenate([angles, angles], axis=1)
    return (jnp.cos(angles), jnp.sin(angles))

def rotate(values, cos_table, sine_table):
    half_dim = values.shape[-1] // 2
    turned = jnp.concatenate([-values[..., half_dim:], values[..., :half_dim]], axis=-1)
    return values * cos_table[:, None, :] + turned * sine_table[:, None, :]

def attend(queries, keys, values, segment):
    row_count = queries.shape[0]
    block_len = min(512, row_count)
    scale_qk = queries.shape[2] ** (-0.5)

    def one_block(offset):
        block_q = lax.dynamic_slice_in_dim(queries, offset, block_len, 0)
        block_seg = lax.dynamic_slice_in_dim(segment, offset, block_len, 0)
        scores = jnp.einsum('qhd,khd->hqk', block_q, keys, precision=precise) * scale_qk
        allowed = block_seg[:, None] == segment[None, :]
        scores = low_back(jnp.where(allowed[None], scores, masked_score))
        attn_probs = low(jax.nn.softmax(scores, axis=-1))
        return low_back(jnp.einsum('hqk,khd->qhd', attn_probs, values, precision=precise))
    offsets = (jnp.arange(row_count // block_len) * block_len).astype(jnp.int32)
    return lax.map(jax.checkpoint(one_block), offsets).reshape(queries.shape)

def block_forward(state, segment, positions, params, layer_idx):
    w_qkv, b_qkv, w_attn_out, w_ff_in, b_ff_in, w_ff_out, out_bias, norm_gain, norm_bias, w_proj = params
    row_count, width = state.shape
    head_count = width // HD
    cos_table, sine_table = rotary_tables(positions, HD)
    inputs = low(state)
    mixed = matmul(inputs, w_qkv[layer_idx].reshape(width, 3 * width)).reshape(row_count, 3, width)
    mixed = low_back(mixed + b_qkv[layer_idx][None])
    head_shape = (row_count, head_count, HD)
    queries = low(rotate(mixed[:, 0].reshape(head_shape), cos_table, sine_table))
    keys = low(rotate(mixed[:, 1].reshape(head_shape), cos_table, sine_table))
    values = low(mixed[:, 2].reshape(head_shape))
    attended = low(attend(queries, keys, values, segment).reshape(row_count, width))
    branch = low_back(matmul(attended, w_attn_out[layer_idx]) + out_bias[layer_idx, 0])
    normed = layer_norm(state + branch, norm_gain[layer_idx, 0], norm_bias[layer_idx, 0])
    upward = low_back(matmul(low(normed), w_ff_in[layer_idx]) + b_ff_in[layer_idx])
    activated = low(jax.nn.gelu(upward, approximate=False))
    branch_ff = low_back(matmul(activated, w_ff_out[layer_idx]) + out_bias[layer_idx, 1])
    return layer_norm(normed + branch_ff, norm_gain[layer_idx, 1], norm_bias[layer_idx, 1])

def encode(params, state, segment, positions):
    for layer_idx in range(LAYERS):
        state = block_forward(state, segment, positions, params, layer_idx)
    projected = matmul(state, params[9])
    return unit(projected)

def reference(doc_hidden, query_hidden, seg_lengths, labels, w_qkv, b_qkv, w_attn_out, w_ff_in, b_ff_in, w_ff_out, out_bias, norm_gain, norm_bias, w_proj):
    params = tuple((array.astype(jnp.float32) for array in (w_qkv, b_qkv, w_attn_out, w_ff_in, b_ff_in, w_ff_out, out_bias, norm_gain, norm_bias, w_proj)))
    docs = doc_hidden.astype(jnp.float32).reshape(N_DP, ROW, D)
    query_group = math.gcd(QUERIES, max(1, 1024 // QLEN))
    group_total = QUERIES // query_group
    query_blocks = query_hidden.astype(jnp.float32).reshape(group_total, query_group * QLEN, D)
    query_place = jnp.arange(query_group * QLEN, dtype=jnp.int32)
    query_segment = query_place // QLEN
    query_position = query_place % QLEN

    def doc_encode(args):
        hidden_row, doc_lens = args
        segment, positions = row_layout(doc_lens, ROW)
        return encode(params, hidden_row, segment, positions)

    def query_encode(hidden_block):
        return encode(params, hidden_block, query_segment, query_position)
    doc_vecs = lax.map(doc_encode, (docs, seg_lengths))
    query_vecs = lax.map(query_encode, query_blocks).reshape(QUERIES, QLEN, DIM)

    def objective(doc_vectors, query_vectors):
        flat_queries = query_vectors.reshape(QUERIES * QLEN, DIM)

        def row_scores(args):
            vectors, doc_lens = args
            segment, _ = row_layout(doc_lens, ROW)
            sims = matmul(flat_queries, vectors.T)
            member = segment[None, :] == jnp.arange(DOCS_ROW, dtype=jnp.int32)[:, None]
            masked = jnp.where(member[None], sims[:, None, :] / tau_token, masked_score)
            soft = jax.nn.logsumexp(masked, axis=-1) - jnp.log(doc_lens.astype(jnp.float32))[None, :]
            return tau_token * soft
        per_row = lax.map(jax.checkpoint(row_scores), (doc_vectors, seg_lengths))
        token_scores = jnp.transpose(per_row, (1, 0, 2)).reshape(QUERIES, QLEN, NDOCS)
        doc_scores = lax.optimization_barrier(jnp.sum(token_scores, axis=1))
        logits = doc_scores / temp_loss
        target = jnp.arange(NDOCS, dtype=jnp.int32)[None, :] == labels[:, None]
        chosen = lax.optimization_barrier(jnp.sum(jnp.where(target, logits, 0.0), axis=1))
        losses = jax.nn.logsumexp(logits, axis=1) - chosen
        return (jnp.sum(losses), losses)
    total, pullback, query_losses = jax.vjp(objective, doc_vecs, query_vecs, has_aux=True)
    doc_cot, query_cot = pullback(jnp.ones_like(total))

    def doc_step(totals, args):
        hidden_row, doc_lens, cotangent = args
        segment, positions = row_layout(doc_lens, ROW)

        def encode_row(weights_in, hidden_in):
            return encode(weights_in, hidden_in, segment, positions)
        _, pull_row = jax.vjp(encode_row, params, hidden_row)
        g_params, g_hidden = pull_row(cotangent)
        return (jax.tree.map(jnp.add, totals, g_params), g_hidden)

    def query_step(totals, args):
        hidden_block, cotangent = args

        def encode_block(weights_in, hidden_in):
            return encode(weights_in, hidden_in, query_segment, query_position)
        _, pull_block = jax.vjp(encode_block, params, hidden_block)
        g_params, g_hidden = pull_block(cotangent)
        return (jax.tree.map(jnp.add, totals, g_params), g_hidden)
    zeros = jax.tree.map(jnp.zeros_like, params)
    grads, g_docs = lax.scan(doc_step, zeros, (docs, seg_lengths, doc_cot))
    grads, g_queries = lax.scan(query_step, grads, (query_blocks, query_cot.reshape(group_total, query_group * QLEN, DIM)))
    return (query_losses, g_docs.reshape(TOKENS, D), g_queries.reshape(QTOKENS, D), grads[0], grads[1], grads[2], grads[3], grads[4], grads[5], grads[6], grads[7], grads[8], grads[9])
```

```python
import math

import jax
import jax.numpy as jnp
from jax import lax
from jax.sharding import PartitionSpec as P

HD = 64
LAYERS = 2

precise = lax.Precision.HIGHEST
eps_norm = 1e-05
eps_unit = 1e-06
tau_token = 0.1
temp_loss = 0.1
masked_score = -1000000000.0
low = jnp.bfloat16


def inner(left, right):
    return lax.dot_general(
        left, right, (((0,), (0,)), ((), ())), preferred_element_type=jnp.float32
    )


def times_t(left, right):
    return lax.dot_general(
        left, right, (((1,), (1,)), ((), ())), preferred_element_type=jnp.float32
    )


def inner_exact(left, right):
    return lax.dot_general(
        left, right, (((0,), (0,)), ((), ())), precision=precise, preferred_element_type=jnp.float32
    )


def times_t_exact(left, right):
    return lax.dot_general(
        left, right, (((1,), (1,)), ((), ())), precision=precise, preferred_element_type=jnp.float32
    )


def layer_norm(values, gain_row, bias_row):
    average = jnp.mean(values, axis=-1, keepdims=True)
    centred = values - average
    spread = jnp.mean(centred * centred, axis=-1, keepdims=True)
    return centred * lax.rsqrt(spread + eps_norm) * gain_row + bias_row


def unit(values):
    return values * lax.rsqrt(jnp.sum(values * values, axis=-1, keepdims=True) + eps_unit)


def gelu_exact(values):
    return jax.nn.gelu(values, approximate=False)


def bits_of(axis):
    size = lax.axis_size(axis)
    assert size & (size - 1) == 0
    return [1 << k for k in reversed(range(size.bit_length() - 1))]


def relative(axis):
    order = [0]
    for bit in bits_of(axis):
        order = order + [one ^ bit for one in order]
    return order


def swap(values, axis, bit):
    return lax.ppermute(values, axis, [(i, i ^ bit) for i in range(lax.axis_size(axis))])


def gather(values, axis):
    for bit in bits_of(axis):
        values = jnp.concatenate([values, swap(values, axis, bit)], axis=0)
    return values


def scatter_sum(values, axis, kind=low):
    for bit in reversed(bits_of(axis)):
        half = values.shape[0] // 2
        taken = swap(values[half:].astype(kind), axis, bit)
        values = values[:half].astype(jnp.float32) + taken.astype(jnp.float32)
    return values


def sum_all(values, axis):
    for bit in reversed(bits_of(axis)):
        values = values + swap(values, axis, bit)
    return values


def own_part(values, index, size):
    return lax.dynamic_slice_in_dim(values, index * size, size, values.ndim - 1)


def arranged(values, own, order):
    size = values.shape[1] // len(order)
    return jnp.concatenate([own_part(values, own ^ step, size) for step in order], axis=1)


def rotary_tables(positions, head_dim):
    half_dim = head_dim // 2
    frequency = jnp.exp(jnp.arange(half_dim, dtype=jnp.float32) * (-math.log(10000.0) / half_dim))
    angles = positions.astype(jnp.float32)[:, None] * frequency[None, :]
    angles = jnp.concatenate([angles, angles], axis=1)
    return (jnp.cos(angles), jnp.sin(angles))


def rotate(values, cos_table, sine_table):
    half_dim = values.shape[-1] // 2
    turned = jnp.concatenate([-values[..., half_dim:], values[..., :half_dim]], axis=-1)
    return values * cos_table[:, None, :] + turned * sine_table[:, None, :]


def rotate_back(grads, cos_table, sine_table):
    half_dim = grads.shape[-1] // 2
    scaled = grads * sine_table[:, None, :]
    turned = jnp.concatenate([scaled[..., half_dim:], -scaled[..., :half_dim]], axis=-1)
    return grads * cos_table[:, None, :] + turned


def masked_scores(queries, keys, segment, scale_qk):
    scores = jnp.einsum("qhd,khd->hqk", queries, keys, preferred_element_type=jnp.float32) * scale_qk
    return jnp.where((segment[:, None] == segment[None, :])[None], scores, masked_score)


def attend_forward(queries, keys, values, segment):
    scores = masked_scores(queries, keys, segment, queries.shape[2] ** (-0.5))
    peak = jnp.max(scores, axis=-1, keepdims=True)
    log_total = peak + jnp.log(jnp.sum(jnp.exp(scores - peak), axis=-1, keepdims=True))
    attn_probs = jnp.exp(scores - log_total).astype(low)
    result = jnp.einsum("hqk,khd->qhd", attn_probs, values, preferred_element_type=jnp.float32)
    return (result, log_total)


def attend_backward(queries, keys, values, segment, log_total, grad_out):
    scale_qk = queries.shape[2] ** (-0.5)
    scores = masked_scores(queries, keys, segment, scale_qk)
    attn_probs = jnp.exp(scores - log_total)
    prob_grad = jnp.einsum("qhd,khd->hqk", grad_out, values, preferred_element_type=jnp.float32)
    delta_row = jnp.sum(attn_probs * prob_grad, axis=-1, keepdims=True)
    score_grad = (attn_probs * (prob_grad - delta_row)).astype(low)
    query_grad = (
        jnp.einsum("hqk,khd->qhd", score_grad, keys, preferred_element_type=jnp.float32) * scale_qk
    )
    key_grad = (
        jnp.einsum("hqk,qhd->khd", score_grad, queries, preferred_element_type=jnp.float32)
        * scale_qk
    )
    value_grad = jnp.einsum(
        "hqk,qhd->khd", attn_probs.astype(low), grad_out, preferred_element_type=jnp.float32
    )
    return (query_grad, key_grad, value_grad)


def layer_forward(state, params, layer_idx, layout):
    w_qkv, b_qkv, w_attn_out, w_ff_in, b_ff_in, w_ff_out, out_bias, norm_gain, norm_bias = params
    segment, cos_table, sine_table = layout
    inputs = gather(state.astype(low), "tensor")
    row_count, width = inputs.shape
    local_width = w_qkv.shape[3]
    mixed = jnp.dot(
        inputs, w_qkv[layer_idx].reshape(width, 3 * local_width), preferred_element_type=jnp.float32
    )
    mixed = mixed.reshape(row_count, 3, local_width) + b_qkv[layer_idx][None]
    head_shape = (row_count, local_width // HD, HD)
    queries = rotate(mixed[:, 0].reshape(head_shape), cos_table, sine_table).astype(low)
    keys = rotate(mixed[:, 1].reshape(head_shape), cos_table, sine_table).astype(low)
    values = mixed[:, 2].reshape(head_shape).astype(low)
    attended, logs = attend_forward(queries, keys, values, segment)
    attended = attended.reshape(row_count, local_width).astype(low)
    branch_terms = jnp.dot(attended, w_attn_out[layer_idx], preferred_element_type=jnp.float32)
    branch = scatter_sum(branch_terms, "tensor")
    residual = state + branch + out_bias[layer_idx, 0]
    normed = layer_norm(residual, norm_gain[layer_idx, 0], norm_bias[layer_idx, 0])
    normed_full = gather(normed.astype(low), "tensor")
    upward = (
        jnp.dot(normed_full, w_ff_in[layer_idx], preferred_element_type=jnp.float32)
        + b_ff_in[layer_idx]
    )
    activated = gelu_exact(upward).astype(low)
    ff_terms = jnp.dot(activated, w_ff_out[layer_idx], preferred_element_type=jnp.float32)
    combined = normed + scatter_sum(ff_terms, "tensor") + out_bias[layer_idx, 1]
    output = layer_norm(combined, norm_gain[layer_idx, 1], norm_bias[layer_idx, 1])
    kept = (inputs, queries, keys, values, logs, attended, residual, normed_full, upward, activated, combined)
    return (output, kept)


def layer_backward(grad_state, kept, params, layer_idx, layout, place):
    w_qkv, b_qkv, w_attn_out, w_ff_in, b_ff_in, w_ff_out, out_bias, norm_gain, norm_bias = params
    segment, cos_table, sine_table = layout
    own_dp, order = place
    (inputs, queries, keys, values, logs, attended, residual, normed_full, upward, activated, combined) = kept
    row_count, width = inputs.shape
    local_width = w_qkv.shape[3]
    _, norm_pull = jax.vjp(layer_norm, combined, norm_gain[layer_idx, 1], norm_bias[layer_idx, 1])
    g_combined, g_gain_ff, g_shift_ff = norm_pull(grad_state)
    g_branch_ff = g_combined.astype(low)
    g_bias_ff = jnp.sum(g_branch_ff, axis=0, dtype=jnp.float32)
    g_ff_full = gather(g_branch_ff, "tensor")
    g_ff_out = scatter_sum(inner(arranged(g_ff_full, own_dp, order), activated), "dp")
    g_activated = times_t(g_ff_full, w_ff_out[layer_idx])
    _, gelu_pull = jax.vjp(gelu_exact, upward)
    g_upward = gelu_pull(g_activated)[0].astype(low)
    g_b_ff_in = jnp.sum(g_upward, axis=0, dtype=jnp.float32)
    ff_back = times_t(g_upward, w_ff_in[layer_idx])
    g_ff_in = scatter_sum(inner(arranged(normed_full, own_dp, order), g_upward), "dp")
    g_normed = g_combined + scatter_sum(ff_back, "tensor")
    _, first_pull = jax.vjp(layer_norm, residual, norm_gain[layer_idx, 0], norm_bias[layer_idx, 0])
    g_residual, g_gain_attn, g_shift_attn = first_pull(g_normed)
    g_branch_attn = g_residual.astype(low)
    g_bias_attn = jnp.sum(g_branch_attn, axis=0, dtype=jnp.float32)
    g_attn_full = gather(g_branch_attn, "tensor")
    g_attn_out = scatter_sum(inner(arranged(g_attn_full, own_dp, order), attended), "dp")
    g_attended = times_t(g_attn_full, w_attn_out[layer_idx]).reshape(queries.shape).astype(low)
    gq, gk, gv = attend_backward(queries, keys, values, segment, logs, g_attended)
    g_queries = rotate_back(gq, cos_table, sine_table)
    g_keys = rotate_back(gk, cos_table, sine_table)
    g_mixed = (
        jnp.stack([g_queries, g_keys, gv], axis=1).reshape(row_count, 3 * local_width).astype(low)
    )
    g_b_qkv = jnp.sum(g_mixed, axis=0, dtype=jnp.float32)
    in_back = times_t(g_mixed, w_qkv[layer_idx].reshape(width, 3 * local_width))
    g_qkv = scatter_sum(inner(arranged(inputs, own_dp, order), g_mixed), "dp")
    g_state = g_residual + scatter_sum(in_back, "tensor")
    g_bias = sum_all(jnp.concatenate([g_b_qkv, g_b_ff_in]), "dp")
    size = local_width // len(order)
    g_b_qkv = own_part(g_bias[: 3 * local_width].reshape(3, local_width), own_dp, size)
    g_b_ff_in = own_part(g_bias[3 * local_width :], own_dp, g_b_ff_in.shape[0] // len(order))
    weight_grads = (
        g_qkv.reshape(g_qkv.shape[0], 3, local_width),
        g_b_qkv,
        g_attn_out.T,
        g_ff_in,
        g_b_ff_in,
        g_ff_out.T,
    )
    small_parts = jnp.stack([g_bias_attn, g_bias_ff, g_gain_attn, g_gain_ff, g_shift_attn, g_shift_ff])
    return (g_state, weight_grads, small_parts)


def per_device(
    doc_hidden,
    query_hidden,
    seg_lengths,
    labels,
    w_qkv,
    b_qkv,
    w_attn_out,
    w_ff_in,
    b_ff_in,
    w_ff_out,
    out_bias,
    norm_gain,
    norm_bias,
    w_proj,
):
    own_dp = lax.axis_index("dp")
    own_tensor = lax.axis_index("tensor")
    dp_size = lax.axis_size("dp")
    tensor_size = lax.axis_size("tensor")
    dp_order = relative("dp")
    tensor_order = relative("tensor")
    share_docs = doc_hidden.shape[0]
    query_len = query_hidden.shape[0]
    share = share_docs + query_len
    doc_lens = seg_lengths[0]
    doc_count = doc_lens.shape[0]
    owner = own_tensor ^ jnp.array(tensor_order, dtype=jnp.int32)
    doc_place = (owner[:, None] * share_docs + jnp.arange(share_docs, dtype=jnp.int32)[None, :])
    doc_ends = jnp.cumsum(doc_lens)
    passed = (doc_place[:, :, None] >= doc_ends[None, None, :]).astype(jnp.int32)
    doc_segment = jnp.sum(passed, axis=2)
    doc_position = doc_place - jnp.sum(passed * doc_lens[None, None, :], axis=2)
    query_segment = jnp.broadcast_to(doc_count + 1 + owner[:, None], (tensor_size, query_len))
    query_position = jnp.broadcast_to(jnp.arange(query_len, dtype=jnp.int32)[None, :], (tensor_size, query_len))
    segment = jnp.concatenate([doc_segment, query_segment], axis=1).reshape(-1)
    positions = jnp.concatenate([doc_position, query_position], axis=1).reshape(-1)
    cos_table, sine_table = rotary_tables(positions, HD)
    layout = (segment, cos_table, sine_table)
    all_labels = gather(labels, "dp")
    params = (w_qkv, b_qkv, w_attn_out, w_ff_in, b_ff_in, w_ff_out, out_bias, norm_gain, norm_bias)
    state = jnp.concatenate([doc_hidden, query_hidden], axis=0).astype(jnp.float32)
    kept_all = []
    for layer_idx in range(LAYERS):
        state, kept = layer_forward(state, params, layer_idx, layout)
        kept_all.append(kept)
    proj_exact = w_proj.astype(jnp.float32)
    projected = jnp.dot(state, proj_exact, precision=precise, preferred_element_type=jnp.float32)
    vectors = unit(projected)
    row_full = gather(vectors[:share_docs], "tensor")
    all_queries = gather(vectors[share_docs:], "dp")
    doc_seg = doc_segment.reshape(-1)
    member = (doc_seg[None, :] == jnp.arange(doc_count, dtype=jnp.int32)[:, None])
    scaled = times_t_exact(all_queries, row_full) / tau_token
    log_list = []
    for doc_pos in range(doc_count):
        masked = jnp.where(member[doc_pos][None, :], scaled, masked_score)
        peak = jnp.max(masked, axis=1)
        log_list.append(peak + jnp.log(jnp.sum(jnp.exp(masked - peak[:, None]), axis=1)))
    log_sums = jnp.stack(log_list, axis=1)
    tok_scores = tau_token * (log_sums - jnp.log(doc_lens.astype(jnp.float32))[None, :])
    query_scores = jnp.sum(tok_scores.reshape(dp_size, query_len, doc_count), axis=1)
    logits = query_scores[None]
    for level, bit in enumerate(bits_of("dp")):
        taken = swap(logits, "dp", bit).reshape(logits.shape[0], -1, 2, 1 << level, doc_count)
        taken = jnp.flip(taken, axis=2).reshape(logits.shape)
        logits = jnp.concatenate([logits, taken], axis=0)
    logits = jnp.swapaxes(logits, 0, 1) / temp_loss
    doc_index = (
        (own_dp ^ jnp.array(dp_order, dtype=jnp.int32))[:, None] * doc_count
        + jnp.arange(doc_count, dtype=jnp.int32)[None, :]
    )
    target = (doc_index[None] == all_labels[:, None, None]).astype(jnp.float32)
    peak = jnp.max(logits, axis=(1, 2), keepdims=True)
    log_total = peak + jnp.log(jnp.sum(jnp.exp(logits - peak), axis=(1, 2), keepdims=True))
    chosen = jnp.sum(target[0] * logits[0])
    query_loss = (log_total[0, 0, 0] - chosen)[None]
    g_groups = (jnp.exp(logits[:, 0] - log_total[:, 0]) - target[:, 0]) / temp_loss
    g_tok = jnp.broadcast_to(g_groups[:, None, :], (dp_size, query_len, doc_count)).reshape(
        dp_size * query_len, doc_count
    )
    member_f = member.astype(jnp.float32)
    log_spread = jnp.dot(log_sums, member_f, precision=precise, preferred_element_type=jnp.float32)
    g_spread = jnp.dot(g_tok, member_f, precision=precise, preferred_element_type=jnp.float32)
    valid = (doc_seg < doc_count)[None, :]
    g_sims = jnp.where(valid, g_spread * jnp.exp(scaled - log_spread), 0.0)
    g_all_queries = jnp.dot(g_sims, row_full, precision=precise, preferred_element_type=jnp.float32)
    g_row_docs = inner_exact(g_sims, all_queries)
    g_doc_vecs = scatter_sum(g_row_docs, "tensor", jnp.float32)
    g_query_vecs = scatter_sum(g_all_queries, "dp", jnp.float32)
    g_vectors = jnp.concatenate([g_doc_vecs, g_query_vecs], axis=0)
    _, unit_pull = jax.vjp(unit, projected)
    g_projected = unit_pull(g_vectors)[0]
    g_w_proj = inner_exact(arranged(state, own_dp, dp_order), g_projected)
    grad_state = times_t_exact(g_projected, proj_exact)
    g_w_proj = sum_all(scatter_sum(g_w_proj, "dp", jnp.float32), "tensor")
    part = g_w_proj.shape[0] // tensor_size
    g_w_proj = lax.dynamic_slice_in_dim(g_w_proj, own_tensor * part, part, 0)
    layer_grads = [None] * LAYERS
    small_list = [None] * LAYERS
    for layer_idx in reversed(range(LAYERS)):
        grad_state, weight_grads, small_parts = layer_backward(
            grad_state, kept_all[layer_idx], params, layer_idx, layout, (own_dp, dp_order)
        )
        layer_grads[layer_idx] = weight_grads
        small_list[layer_idx] = small_parts
    stacked = tuple(
        (
            jnp.stack([layer_grads[layer_pos][member_pos] for layer_pos in range(LAYERS)])
            for member_pos in range(6)
        )
    )
    small = sum_all(sum_all(jnp.stack(small_list), "tensor"), "dp")
    part = small.shape[2] // (dp_size * tensor_size)
    small = own_part(small, own_dp * tensor_size + own_tensor, part)
    return (
        query_loss,
        grad_state[:share_docs],
        grad_state[share_docs:],
        stacked[0],
        stacked[1],
        stacked[2],
        stacked[3],
        stacked[4],
        stacked[5],
        small[:, 0:2],
        small[:, 2:4],
        small[:, 4:6],
        g_w_proj,
    )


def solution(mesh):
    return jax.shard_map(
        per_device,
        mesh=mesh,
        in_specs=(
            P(("dp", "tensor"), None),
            P(("dp", "tensor"), None),
            P("dp", None),
            P(("dp", "tensor")),
            P(None, None, None, "tensor"),
            P(None, None, "tensor"),
            P(None, "tensor", None),
            P(None, None, "tensor"),
            P(None, "tensor"),
            P(None, "tensor", None),
            P(),
            P(),
            P(),
            P(),
        ),
        out_specs=(
            P(("dp", "tensor")),
            P(("dp", "tensor"), None),
            P(("dp", "tensor"), None),
            P(None, "dp", None, "tensor"),
            P(None, None, ("tensor", "dp")),
            P(None, "tensor", "dp"),
            P(None, "dp", "tensor"),
            P(None, ("tensor", "dp")),
            P(None, "tensor", "dp"),
            P(None, None, ("dp", "tensor")),
            P(None, None, ("dp", "tensor")),
            P(None, None, ("dp", "tensor")),
            P(("dp", "tensor"), None),
        ),
        check_vma=False,
    )
```

```python
import math

import jax
import jax.numpy as jnp
from jax import lax
from jax.experimental import pallas as pl
from jax.experimental.pallas import tpu as pltpu
from jax.sharding import PartitionSpec as P

HD = 64
LAYERS = 2
MIB = 1 << 20

precise = lax.Precision.HIGHEST
eps_norm = 1e-05
eps_unit = 1e-06
tau_token = 0.1
temp_loss = 0.1
masked_score = -1000000000.0
low = jnp.bfloat16
f32 = jnp.float32


def nn(a, b):
    return lax.dot_general(a, b, (((1,), (0,)), ((), ())), preferred_element_type=f32)
def nt(a, b):
    return lax.dot_general(a, b, (((1,), (1,)), ((), ())), preferred_element_type=f32)
def tn(a, b):
    return lax.dot_general(a, b, (((0,), (0,)), ((), ())), preferred_element_type=f32)

def call(body, outs, scratch=(), limit=24, flops=0, bytes_=0):
    return pl.pallas_call(
        body,
        out_shape=[jax.ShapeDtypeStruct(s, d) for s, d in outs],
        scratch_shapes=list(scratch),
        compiler_params=pltpu.CompilerParams(vmem_limit_bytes=limit * MIB),
        cost_estimate=pl.CostEstimate(flops=flops, bytes_accessed=bytes_, transcendentals=0),
    )

def erf(x):
    x = jnp.clip(x, -3.832506856900711, 3.832506856900711)
    x2 = x * x
    p = 0.00022905065861350646
    for c in (0.0034082910107109506, 0.050955695062380861, 0.18520832239976145, 1.128379143519084):
        p = p * x2 + c
    q = -1.1791602954361697e-7
    for c in (0.000023547966471313185, 0.0010179625278914885, 0.014070470171167667, 0.11098505178285362, 0.49746925110067538, 1.0):
        q = q * x2 + c
    return x * p / q

def put(full, pieces, docs, total_docs):
    for p, piece in enumerate(pieces):
        n = piece.shape[0] - docs
        full[p * docs:(p + 1) * docs, :] = piece[:docs, :]
        full[total_docs + p * n: total_docs + (p + 1) * n, :] = piece[docs:, :]

def turned(v, first):
    w = v.shape[1]
    return jnp.where(first, -pltpu.roll(v, w - 32, 1), pltpu.roll(v, 32, 1))

def first_half(shape):
    return (lax.broadcasted_iota(jnp.int32, shape, 1) & 63) < 32


def qkv_attention(pieces, w_qkv, b_qkv, cos, sin, seg_row, seg_col, w_out, docs):
    count = len(pieces)
    share, width = pieces[0].shape
    queries = share - docs
    n_docs, n_q = docs * count, queries * count
    rows = n_docs + n_q
    local = w_out.shape[0]
    pairs = local // 128

    def body(*refs):
        xs = refs[:count]
        w, b, cos_r, sin_r, srow, scol, wo, full, q_s, k_s, v_s, att, far, near, mine, att_t, terms = refs[count:]
        put(full, xs, docs, n_docs)
        cos_v = jnp.concatenate([cos_r[...]] * pairs, axis=1)
        sin_v = jnp.concatenate([sin_r[...]] * pairs, axis=1)
        first = first_half((rows, local))
        for j, dst in enumerate((q_s, k_s, v_s)):
            m = nn(full[...], w[:, j * local:(j + 1) * local]) + b[:, j * local:(j + 1) * local]
            if j < 2:
                m = m * cos_v + turned(m, first) * sin_v
            m = m.astype(low)
            for p in range(pairs):
                dst[p] = m[:, p * 128:(p + 1) * 128]
        doc_mask = scol[...] == srow[...]
        at = lax.broadcasted_iota(jnp.int32, (n_q, n_q), 0) // queries
        to = lax.broadcasted_iota(jnp.int32, (n_q, n_q), 1) // queries
        query_mask = at == to

        def pair(p, _):
            for start, size, mask in ((0, n_docs, doc_mask), (n_docs, n_q, query_mask)):
                outs = []
                for h in range(2):
                    lanes = slice(h * HD, (h + 1) * HD)
                    qh = q_s[p, start:start + size, lanes] * jnp.asarray(HD ** -0.5, low)
                    kh = k_s[p, start:start + size, lanes]
                    vh = v_s[p, start:start + size, lanes]
                    s = jnp.where(mask, nt(kh, qh), masked_score)
                    e = jnp.exp(s - jnp.max(s, axis=0, keepdims=True))
                    pr = (e * (1.0 / jnp.sum(e, axis=0, keepdims=True))).astype(low)
                    outs.append(tn(vh, pr))
                att_t[p, :, start:start + size] = jnp.concatenate(outs, axis=0)
            return 0

        lax.fori_loop(0, pairs, pair, 0)
        for p in range(pairs):
            att[:, p * 128:(p + 1) * 128] = att_t[p].T.astype(low)
        terms[...] = nn(att[...], wo[...])
        hand_out(terms, far, near, mine, docs, n_docs, count)

    half = count // 2
    outs = [((rows, width), low)] + [((pairs, rows, 128), low)] * 3 + [((rows, local), low)] + sum_shapes(share, width, count)
    return call(
        body, outs, [pltpu.VMEM((pairs, 128, rows), f32), pltpu.VMEM((rows, width), f32)], limit=28,
        flops=2 * rows * width * local * 4, bytes_=8 * MIB,
    )(*pieces, w_qkv, b_qkv, cos, sin, seg_row, seg_col, w_out)


def sum_shapes(share, width, count):
    half = count // 2
    return [((half * share, width), low), (((half - 1) * share, width), f32), ((share, width), f32)]


def hand_out(terms, far, near, mine, docs, n_docs, count):
    share = mine.shape[0]
    queries = share - docs
    half = count // 2
    for p in range(count):
        dst, at = (mine, 0) if p == 0 else (near, p - 1) if p < half else (far, p - half)
        dst[at * share: at * share + docs, :] = terms[p * docs:(p + 1) * docs, :].astype(dst.dtype)
        dst[at * share + docs:(at + 1) * share, :] = terms[n_docs + p * queries: n_docs + (p + 1) * queries, :].astype(dst.dtype)


def ff_forward(pieces, w_in, b_in, w_out, docs):
    count = len(pieces)
    share, width = pieces[0].shape
    n_docs = docs * count
    rows = share * count
    local = w_out.shape[0]
    tile = 256

    def body(*refs):
        xs = refs[:count]
        wi, b, wo, full, up, act, far, near, mine, terms = refs[count:]
        put(full, xs, docs, n_docs)

        def columns(j, _):
            at = pl.ds(pl.multiple_of(j * tile, tile), tile)
            u = nn(full[...], wi[:, at]) + b[:, at]
            up[:, at] = u
            act[:, at] = (0.5 * u * (1.0 + erf(u * (0.5 ** 0.5)))).astype(low)
            return 0

        lax.fori_loop(0, local // tile, columns, 0)
        terms[...] = nn(act[...], wo[...])
        hand_out(terms, far, near, mine, docs, n_docs, count)

    outs = [((rows, width), low), ((rows, local), f32), ((rows, local), low)] + sum_shapes(share, width, count)
    return call(body, outs, [pltpu.VMEM((rows, width), f32)], limit=28, flops=4 * rows * width * local, bytes_=12 * MIB)(
        *pieces, w_in, b_in, w_out
    )


def gelu_slope(up):
    def body(u_ref, o_ref):
        u = u_ref[...]
        o_ref[...] = (0.5 * (1.0 + erf(u * (0.5 ** 0.5))) + u * (jnp.exp(-0.5 * u * u) * (2.0 * math.pi) ** -0.5)).astype(low)
    return call(body, [(up.shape, low)], limit=12, flops=up.size * 60, bytes_=up.size * 6)(up)[0]


def norm_forward(state, mine, near_sum, far_sum, bias, gain, shift):
    share, width = state.shape

    def body(x, a, b, c, ob, g, s, out, out_low, hat, scale):
        y = x[...].astype(f32) + a[...] + b[:share, :].astype(f32) + c[...].astype(f32) + ob[...]
        mean = jnp.mean(y, axis=1, keepdims=True)
        centred = y - mean
        r = lax.rsqrt(jnp.mean(centred * centred, axis=1, keepdims=True) + eps_norm)
        h = centred * r
        hat[...] = h
        scale[...] = jnp.broadcast_to(r, scale.shape)
        n = h * g[...] + s[...]
        out[...] = n
        out_low[...] = n.astype(low)

    outs = [((share, width), f32), ((share, width), low), ((share, width), f32), ((share, 128), f32)]
    return call(body, outs, limit=12, flops=share * width * 10, bytes_=share * width * 20)(state, mine, near_sum, far_sum, bias, gain, shift)


def norm_backward(grad, parts, hat, scale, gain):
    share, width = hat.shape

    def body(*refs):
        g = refs[0][...]
        ps = refs[1:1 + len(parts)]
        if ps:
            g = g + ps[0][...] + ps[1][:share, :].astype(f32) + ps[2][...].astype(f32)
        hat_r, scale_r, gain_r, out, out_low, sums = refs[1 + len(parts):]
        h = hat_r[...]
        gg = g * gain_r[...]
        r = scale_r[:, :1]
        d = r * (gg - jnp.mean(gg, axis=1, keepdims=True) - h * jnp.mean(gg * h, axis=1, keepdims=True))
        dl = d.astype(low)
        out[...] = d
        out_low[...] = dl
        sums[0:1, :] = jnp.sum(dl.astype(f32), axis=0, keepdims=True)
        sums[1:2, :] = jnp.sum(g * h, axis=0, keepdims=True)
        sums[2:3, :] = jnp.sum(g, axis=0, keepdims=True)
        sums[3:8, :] = jnp.zeros((5, width), f32)

    outs = [((share, width), f32), ((share, width), low), ((8, width), f32)]
    return call(body, outs, limit=12, flops=share * width * 14, bytes_=share * width * 20)(grad, *parts, hat, scale, gain)


def ff_backward(pieces, slope, w_in, w_out, docs):
    count = len(pieces)
    share, width = pieces[0].shape
    n_docs = docs * count
    rows = share * count
    local = w_out.shape[0]
    tile = 256

    def body(*refs):
        xs = refs[:count]
        sl, wi, wo, full, gu, sums, far, near, mine, terms = refs[count:]
        put(full, xs, docs, n_docs)

        def columns(j, _):
            at = pl.ds(pl.multiple_of(j * tile, tile), tile)
            g = (nt(full[...], wo[at, :]) * sl[:, at].astype(f32)).astype(low)
            gu[:, at] = g
            sums[:, at] = jnp.broadcast_to(jnp.sum(g.astype(f32), axis=0, keepdims=True), (8, tile))
            return 0

        lax.fori_loop(0, local // tile, columns, 0)
        terms[...] = nt(gu[...], wi[...])
        hand_out(terms, far, near, mine, docs, n_docs, count)

    outs = [((rows, width), low), ((rows, local), low), ((8, local), f32)] + sum_shapes(share, width, count)
    return call(body, outs, [pltpu.VMEM((rows, width), f32)], limit=28, flops=4 * rows * width * local, bytes_=10 * MIB)(
        *pieces, slope, w_in, w_out
    )


def attention_backward(pieces, q, k, v, cos, sin, seg_row, seg_col, w_qkv, w_out, docs):
    count = len(pieces)
    share, width = pieces[0].shape
    queries = share - docs
    n_docs, n_q = docs * count, queries * count
    rows = n_docs + n_q
    local = w_out.shape[0]
    pairs = local // 128
    scale = HD ** -0.5

    def body(*refs):
        xs = refs[:count]
        (q_s, k_s, v_s, cos_r, sin_r, srow, scol, w, wo, full, gm, sums, far, near, mine, go, gq_t, gk, terms) = refs[count:]
        put(full, xs, docs, n_docs)
        g = nt(full[...], wo[...]).astype(low)
        for p in range(pairs):
            go[p] = g[:, p * 128:(p + 1) * 128]
        doc_mask = scol[...] == srow[...]
        at = lax.broadcasted_iota(jnp.int32, (n_q, n_q), 0) // queries
        to = lax.broadcasted_iota(jnp.int32, (n_q, n_q), 1) // queries
        query_mask = at == to

        def pair(p, _):
            for start, size, mask in ((0, n_docs, doc_mask), (n_docs, n_q, query_mask)):
                gqs, gks, gvs = [], [], []
                for h in range(2):
                    lanes = slice(h * HD, (h + 1) * HD)
                    qh = q_s[p, start:start + size, lanes] * jnp.asarray(scale, low)
                    kh = k_s[p, start:start + size, lanes]
                    vh = v_s[p, start:start + size, lanes]
                    gh = go[p, start:start + size, lanes]
                    s = jnp.where(mask, nt(kh, qh), masked_score)
                    e = jnp.exp(s - jnp.max(s, axis=0, keepdims=True))
                    pr = e * (1.0 / jnp.sum(e, axis=0, keepdims=True))
                    gp = nt(vh, gh)
                    gs = (pr * (gp - jnp.sum(pr * gp, axis=0, keepdims=True))).astype(low)
                    gvs.append(nn(pr.astype(low), gh))
                    gks.append(nn(gs, qh))
                    gqs.append(tn(kh, gs) * scale)
                gq_t[p, :, start:start + size] = jnp.concatenate(gqs, axis=0)
                gk[0, p, start:start + size, :] = jnp.concatenate(gks, axis=1)
                gk[1, p, start:start + size, :] = jnp.concatenate(gvs, axis=1)
            return 0

        lax.fori_loop(0, pairs, pair, 0)
        first = first_half((rows, 128))
        for j in range(3):
            for p in range(pairs):
                m = gq_t[p].T if j == 0 else gk[j - 1, p]
                if j < 2:
                    m = m * cos_r[...] - turned(m, first) * sin_r[...]
                m = m.astype(low)
                lo = j * local + p * 128
                gm[:, lo:lo + 128] = m
                sums[:, lo:lo + 128] = jnp.broadcast_to(jnp.sum(m.astype(f32), axis=0, keepdims=True), (8, 128))
        terms[...] = nt(gm[...], w[...])
        hand_out(terms, far, near, mine, docs, n_docs, count)

    outs = [((rows, width), low), ((rows, 3 * local), low), ((8, 3 * local), f32)] + sum_shapes(share, width, count)
    scratch = [
        pltpu.VMEM((pairs, rows, 128), low), pltpu.VMEM((pairs, 128, rows), f32),
        pltpu.VMEM((2, pairs, rows, 128), f32), pltpu.VMEM((rows, width), f32),
    ]
    return call(body, outs, scratch, limit=32, flops=2 * rows * width * local * 6, bytes_=10 * MIB)(
        *pieces, q, k, v, cos, sin, seg_row, seg_col, w_qkv, w_out
    )


def weight_grads(own, order, products):
    rows, width = products[0][0].shape
    total = sum(r.shape[1] for _, r in products)
    widest = max(r.shape[1] for _, r in products)
    size = width // len(order)
    tall = max(size, 128)
    group = tall // size
    half = len(order) // 2
    place = {step: j for j, step in enumerate(order)}

    def body(own_ref, *refs):
        keep, send = refs[2 * len(products) : 2 * len(products) + 2]
        me = own_ref[0]
        at = 0
        for i in range(len(products)):
            left, right = refs[2 * i], refs[2 * i + 1]
            n = right.shape[1]

            def put_block(step, value):
                j = place[step]
                dst, j = (send, j - half) if j >= half else (keep, j)
                dst[j * size : (j + 1) * size, at : at + n] = value.astype(dst.dtype)

            for first in sorted(range(0, len(order), group), key=lambda step: -place[step]):
                block = pl.multiple_of(((me // group) ^ (first // group)) * tall, tall)
                value = tn(left[:, pl.ds(block, tall)], right[...])
                if group == 1:
                    put_block(first, value)
                    continue
                held = refs[-1]
                held[:, :n] = value
                for one in range(group):
                    sub = pl.multiple_of(((me % group) ^ one) * size, size)
                    put_block(first + one, held[pl.ds(sub, size), :n])
            at += n

    flat = [a for pair in products for a in pair]
    return pl.pallas_call(
        body,
        out_shape=[jax.ShapeDtypeStruct((width // 2, total), f32), jax.ShapeDtypeStruct((width // 2, total), low)],
        in_specs=[pl.BlockSpec(memory_space=pltpu.SMEM)] + [pl.BlockSpec(memory_space=pltpu.VMEM)] * len(flat),
        scratch_shapes=[pltpu.VMEM((tall, widest), f32)] if group > 1 else [],
        compiler_params=pltpu.CompilerParams(vmem_limit_bytes=28 * MIB),
        cost_estimate=pl.CostEstimate(
            flops=2 * rows * width * total,
            bytes_accessed=width * total * 3 + rows * (2 * width + total) * 2,
            transcendentals=0,
        ),
    )(own, *flat)


def inner_exact(left, right):
    return lax.dot_general(
        left, right, (((0,), (0,)), ((), ())), precision=precise, preferred_element_type=f32
    )


def times_t_exact(left, right):
    return lax.dot_general(
        left, right, (((1,), (1,)), ((), ())), precision=precise, preferred_element_type=f32
    )


def unit(values):
    return values * lax.rsqrt(jnp.sum(values * values, axis=-1, keepdims=True) + eps_unit)


def bits_of(axis):
    size = lax.axis_size(axis)
    assert size & (size - 1) == 0
    return [1 << k for k in reversed(range(size.bit_length() - 1))]


def relative(axis):
    order = [0]
    for bit in bits_of(axis):
        order = order + [one ^ bit for one in order]
    return order


def swap(values, axis, bit):
    return lax.ppermute(values, axis, [(i, i ^ bit) for i in range(lax.axis_size(axis))])


def gather(values, axis):
    for bit in bits_of(axis):
        values = jnp.concatenate([values, swap(values, axis, bit)], axis=0)
    return values


def gather_pieces(values):
    pieces = [values]
    for bit in bits_of("tensor"):
        pieces = pieces + [swap(piece, "tensor", bit) for piece in pieces]
    return pieces


def reduce_pieces(far, near, mine):
    share = mine.shape[0]
    taken = swap(far, "tensor", 1)
    other = swap((near + taken[share:].astype(f32)).astype(low), "tensor", 2)
    return (mine, taken, other)


def scatter_sum(values, axis, kind=low):
    for bit in reversed(bits_of(axis)):
        half = values.shape[0] // 2
        taken = swap(values[half:].astype(kind), axis, bit)
        values = values[:half].astype(f32) + taken.astype(f32)
    return values


def scatter_halves(keep, send):
    bits = list(reversed(bits_of("dp")))
    for at, bit in enumerate(bits):
        taken = swap(send, "dp", bit).astype(f32)
        if at == len(bits) - 1:
            return keep + taken
        half = keep.shape[0] // 2
        send = (keep[half:] + taken[half:]).astype(low)
        keep = keep[:half] + taken[:half]


def sum_all(values, axis):
    for bit in reversed(bits_of(axis)):
        values = values + swap(values, axis, bit)
    return values


def own_part(values, index, size):
    return lax.dynamic_slice_in_dim(values, index * size, size, values.ndim - 1)


def arranged(values, own, order):
    size = values.shape[1] // len(order)
    return jnp.concatenate([own_part(values, own ^ step, size) for step in order], axis=1)


def rotary_tables(positions):
    half_dim = HD // 2
    frequency = jnp.exp(jnp.arange(half_dim, dtype=f32) * (-math.log(10000.0) / half_dim))
    angles = positions.astype(f32)[:, None] * jnp.tile(frequency, 4)[None, :]
    return (jnp.cos(angles), jnp.sin(angles))


def per_device(
    doc_hidden,
    query_hidden,
    seg_lengths,
    labels,
    w_qkv,
    b_qkv,
    w_attn_out,
    w_ff_in,
    b_ff_in,
    w_ff_out,
    out_bias,
    norm_gain,
    norm_bias,
    w_proj,
):
    own_dp = lax.axis_index("dp")
    own_tensor = lax.axis_index("tensor")
    dp_size = lax.axis_size("dp")
    tensor_size = lax.axis_size("tensor")
    dp_order = relative("dp")
    share_docs = doc_hidden.shape[0]
    query_len = query_hidden.shape[0]
    width = doc_hidden.shape[1]
    local = w_attn_out.shape[1]
    own = own_dp[None].astype(jnp.int32)
    state = jnp.concatenate([doc_hidden, query_hidden], axis=0)
    pieces = gather_pieces(state)
    doc_lens = seg_lengths[0]
    doc_count = doc_lens.shape[0]
    owner = own_tensor ^ jnp.array(relative("tensor"), dtype=jnp.int32)
    doc_place = (owner[:, None] * share_docs + jnp.arange(share_docs, dtype=jnp.int32)[None, :]).reshape(-1)
    doc_ends = jnp.cumsum(doc_lens)
    passed = (doc_place[:, None] >= doc_ends[None, :]).astype(jnp.int32)
    doc_seg = jnp.sum(passed, axis=1)
    doc_position = doc_place - jnp.sum(passed * doc_lens[None, :], axis=1)
    query_position = jnp.arange(query_len * tensor_size, dtype=jnp.int32) % query_len
    cos_table, sine_table = rotary_tables(jnp.concatenate([doc_position, query_position]))
    layout = (cos_table, sine_table, doc_seg[None, :], doc_seg[:, None])
    w_mix = [w_qkv[i].reshape(width, 3 * local) for i in range(LAYERS)]
    saved = []
    for i in range(LAYERS):
        full, q, k, v, attended, *sums = qkv_attention(
            pieces, w_mix[i], b_qkv[i].reshape(1, 3 * local), *layout, w_attn_out[i], share_docs
        )
        normed, normed_low, hat_attn, scale_attn = norm_forward(
            state, *reduce_pieces(*sums), out_bias[i, 0][None], norm_gain[i, 0][None], norm_bias[i, 0][None]
        )
        normed_full, upward, activated, *sums = ff_forward(
            gather_pieces(normed_low), w_ff_in[i], b_ff_in[i][None], w_ff_out[i], share_docs
        )
        slope = gelu_slope(upward)
        state, state_low, hat_ff, scale_ff = norm_forward(
            normed, *reduce_pieces(*sums), out_bias[i, 1][None], norm_gain[i, 1][None], norm_bias[i, 1][None]
        )
        if i < LAYERS - 1:
            pieces = gather_pieces(state_low)
        saved.append((full, q, k, v, attended, hat_attn, scale_attn, normed_full, slope, activated, hat_ff, scale_ff))
    proj_exact = w_proj.astype(f32)
    projected = jnp.dot(state, proj_exact, precision=precise, preferred_element_type=f32)
    vectors = unit(projected)
    row_full = gather(vectors[:share_docs], "tensor")
    all_queries = gather(vectors[share_docs:], "dp")
    member = doc_seg[None, :] == jnp.arange(doc_count, dtype=jnp.int32)[:, None]
    scaled = times_t_exact(all_queries, row_full) / tau_token
    log_list = []
    for doc_pos in range(doc_count):
        masked = jnp.where(member[doc_pos][None, :], scaled, masked_score)
        peak = jnp.max(masked, axis=1)
        log_list.append(peak + jnp.log(jnp.sum(jnp.exp(masked - peak[:, None]), axis=1)))
    log_sums = jnp.stack(log_list, axis=1)
    tok_scores = tau_token * (log_sums - jnp.log(doc_lens.astype(f32))[None, :])
    query_scores = jnp.sum(tok_scores.reshape(dp_size, query_len, doc_count), axis=1)
    logits = jnp.concatenate([query_scores, jnp.broadcast_to(labels.astype(f32)[:, None], (dp_size, 1))], axis=1)[None]
    for level, bit in enumerate(bits_of("dp")):
        taken = swap(logits, "dp", bit).reshape(logits.shape[0], -1, 2, 1 << level, doc_count + 1)
        taken = jnp.flip(taken, axis=2).reshape(logits.shape)
        logits = jnp.concatenate([logits, taken], axis=0)
    all_labels = logits[:, 0, doc_count]
    logits = jnp.swapaxes(logits[:, :, :doc_count], 0, 1) / temp_loss
    doc_index = (
        (own_dp ^ jnp.array(dp_order, dtype=jnp.int32))[:, None] * doc_count
        + jnp.arange(doc_count, dtype=jnp.int32)[None, :]
    ).astype(f32)
    target = (doc_index[None] == all_labels[:, None, None]).astype(f32)
    peak = jnp.max(logits, axis=(1, 2), keepdims=True)
    log_total = peak + jnp.log(jnp.sum(jnp.exp(logits - peak), axis=(1, 2), keepdims=True))
    chosen = jnp.sum(target[0] * logits[0])
    query_loss = (log_total[0, 0, 0] - chosen)[None]
    g_groups = (jnp.exp(logits[:, 0] - log_total[:, 0]) - target[:, 0]) / temp_loss
    g_tok = jnp.broadcast_to(g_groups[:, None, :], (dp_size, query_len, doc_count)).reshape(
        dp_size * query_len, doc_count
    )
    member_f = member.astype(f32)
    log_spread = jnp.dot(log_sums, member_f, precision=precise, preferred_element_type=f32)
    g_spread = jnp.dot(g_tok, member_f, precision=precise, preferred_element_type=f32)
    valid = (doc_seg < doc_count)[None, :]
    g_sims = jnp.where(valid, g_spread * jnp.exp(scaled - log_spread), 0.0)
    g_all_queries = jnp.dot(g_sims, row_full, precision=precise, preferred_element_type=f32)
    g_row_docs = inner_exact(g_sims, all_queries)
    g_doc_vecs = scatter_sum(g_row_docs, "tensor", f32)
    g_query_vecs = scatter_sum(g_all_queries, "dp", f32)
    g_vectors = jnp.concatenate([g_doc_vecs, g_query_vecs], axis=0)
    _, unit_pull = jax.vjp(unit, projected)
    g_projected = unit_pull(g_vectors)[0]
    g_w_proj = inner_exact(arranged(state, own_dp, dp_order), g_projected)
    grad = times_t_exact(g_projected, proj_exact)
    g_w_proj = sum_all(scatter_sum(g_w_proj, "dp", f32), "tensor")
    part = g_w_proj.shape[0] // tensor_size
    g_w_proj = lax.dynamic_slice_in_dim(g_w_proj, own_tensor * part, part, 0)
    grads = [None] * LAYERS
    small = [None] * LAYERS
    biases = [None] * LAYERS
    parts = ()
    for i in reversed(range(LAYERS)):
        full, q, k, v, attended, hat_attn, scale_attn, normed_full, slope, activated, hat_ff, scale_ff = saved[i]
        grad, grad_low, small_ff = norm_backward(grad, parts, hat_ff, scale_ff, norm_gain[i, 1][None])
        grad_full, g_up, b_up, *sums = ff_backward(gather_pieces(grad_low), slope, w_ff_in[i], w_ff_out[i], share_docs)
        g_ff = scatter_halves(*weight_grads(own, dp_order, [(normed_full, g_up), (grad_full, activated)]))
        grad, grad_low, small_attn = norm_backward(
            grad, reduce_pieces(*sums), hat_attn, scale_attn, norm_gain[i, 0][None]
        )
        grad_full, g_mix, b_mix, *sums = attention_backward(
            gather_pieces(grad_low), q, k, v, *layout, w_mix[i], w_attn_out[i], share_docs
        )
        g_attn = scatter_halves(*weight_grads(own, dp_order, [(full, g_mix), (grad_full, attended)]))
        parts = reduce_pieces(*sums)
        hidden = activated.shape[1]
        grads[i] = (g_attn[:, : 3 * local].reshape(-1, 3, local), g_attn[:, 3 * local :].T, g_ff[:, :hidden], g_ff[:, hidden:].T)
        small[i] = [jnp.stack([small_attn[j], small_ff[j]]) for j in range(3)]
        biases[i] = jnp.concatenate([b_mix[0], b_up[0]])
    grad = grad + parts[0] + parts[1][: grad.shape[0]].astype(f32) + parts[2].astype(f32)
    small = jnp.stack([jnp.stack(one) for one in small])
    small = sum_all(sum_all(small, "tensor"), "dp")
    small = own_part(small, own_dp * tensor_size + own_tensor, width // (dp_size * tensor_size))
    biases = sum_all(jnp.stack(biases), "dp")
    g_b_qkv = own_part(biases[:, : 3 * local].reshape(LAYERS, 3, local), own_dp, local // dp_size)
    g_b_ff_in = own_part(biases[:, 3 * local :], own_dp, (biases.shape[1] - 3 * local) // dp_size)
    g_qkv, g_attn_out, g_ff_in, g_ff_out = (jnp.stack([grads[i][j] for i in range(LAYERS)]) for j in range(4))
    return (
        query_loss,
        grad[:share_docs],
        grad[share_docs:],
        g_qkv,
        g_b_qkv,
        g_attn_out,
        g_ff_in,
        g_b_ff_in,
        g_ff_out,
        small[:, 0],
        small[:, 1],
        small[:, 2],
        g_w_proj,
    )


def solution(mesh):
    return jax.shard_map(
        per_device,
        mesh=mesh,
        in_specs=(
            P(("dp", "tensor"), None),
            P(("dp", "tensor"), None),
            P("dp", None),
            P(("dp", "tensor")),
            P(None, None, None, "tensor"),
            P(None, None, "tensor"),
            P(None, "tensor", None),
            P(None, None, "tensor"),
            P(None, "tensor"),
            P(None, "tensor", None),
            P(),
            P(),
            P(),
            P(),
        ),
        out_specs=(
            P(("dp", "tensor")),
            P(("dp", "tensor"), None),
            P(("dp", "tensor"), None),
            P(None, "dp", None, "tensor"),
            P(None, None, ("tensor", "dp")),
            P(None, "tensor", "dp"),
            P(None, "dp", "tensor"),
            P(None, ("tensor", "dp")),
            P(None, "tensor", "dp"),
            P(None, None, ("dp", "tensor")),
            P(None, None, ("dp", "tensor")),
            P(None, None, ("dp", "tensor")),
            P(("dp", "tensor"), None),
        ),
        check_vma=False,
    )
```
